32 devices in a mesh: parts: 2 (over y), seq: 4 (over z), fsdp: 2 (over x), chan: 2 (over core).
Axes of the slice: x: 2, y: 2, z: 4, core: 2. Of those that a mesh axis runs over, the one named last changes fastest.
Arguments:
- ids: int32 [3072], P(('parts', 'seq')), parts along dimension 0, may hold values from 0 to 511
- embed: bfloat16 [512, 4096], replicated, may hold values from -6 to 6
- norm_gain: float32 [4096], replicated, may hold values from 0.1 to 1.9
- w_in: bfloat16 [4096, 3, 4096], P('seq', None, ('fsdp', 'chan')), may hold values from -0.09375 to 0.09375
- short_filter: float32 [3, 3, 4096], P(None, None, ('fsdp', 'chan')), may hold values from -3 to 3
- long_filter: float32 [256, 128], P(('fsdp', 'chan')), may hold values from -1 to 1
- skip_bias: float32 [4096], P(('fsdp', 'chan')), may hold values from -4 to 4
- w_out: bfloat16 [4096, 4096], P('seq', ('fsdp', 'chan')), may hold values from -0.09375 to 0.09375
Outputs:
- block_out: bfloat16 [3072, 4096], P(('parts', 'seq'), ('fsdp', 'chan')), parts along dimension 0
The draws below stay inside these ranges and needn't reach their ends.
There are 2 independent parts, one for each index of `parts`. The reference program is written for one: setup_inputs(seed, part) draws one part's arguments, and reference() takes and returns one part's arrays. A program takes and returns all parts, laid end to end along the dimension named above; an argument that names none is the same for every part. Nothing has to cross between parts.
All inputs are finite; a program needn't handle non-finite values.
Results may differ from the reference program's by a relative error of at most 0.0082.
Values may be sent and summed in bfloat16 or wider, within the bound.
A program may use at most 128 MiB of HBM per device.

```python
import math
import jax
import jax.numpy as jnp
import numpy as np
from jax import lax

D = 4096
GROUPS = 256
FL = 128
SHORT = 3
VOCAB = 512
SEQ_LEN = 1536


def touch_ends(array, rng, least, high):
    extent = array.shape
    place = [jax.random.randint(jax.random.fold_in(rng, axis), (), 0, extent[axis]) for axis in range(len(extent))]
    array = array.at[tuple(place)].set(least)
    longest = extent.index(max(extent))
    place[longest] = (place[longest] + 1) % extent[longest]
    return array.at[tuple(place)].set(high)


def level_of(stream_key, shape, pieces, least, high):
    level, own = 1.0, jax.random.fold_in(stream_key, 6)
    for dim, blocks in pieces:
        steps = jnp.exp(jax.random.uniform(jax.random.fold_in(own, dim), (blocks,), jnp.float32, least / len(pieces), high / len(pieces)))
        level = level * jnp.repeat(steps, shape[dim] // blocks).reshape([-1 if axis == dim else 1 for axis in range(len(shape))])
    return level


def cumulative_ranks(count, slope):
    weights = [(1 << 20) // math.isqrt(grade ** slope) + 1 for grade in range(1, count + 1)]
    width = 1 + sum(weights) // (1 << 30)
    return np.cumsum(np.array([max(1, weight // width) for weight in weights]))


def ranked(rng, dims, number_of, lean):
    listing = cumulative_ranks(number_of, lean)
    lot = jax.random.randint(jax.random.fold_in(rng, 1), dims, 0, int(listing[number_of - 1]))
    rank = jnp.searchsorted(jnp.asarray(listing, jnp.int32), lot, side="right")
    return jax.random.permutation(jax.random.fold_in(rng, 2), number_of)[rank].astype(jnp.int32)


def bell_draw(own_key, shape, deviation, bound, split=(), kind=jnp.bfloat16):
    result = deviation * jax.random.normal(own_key, shape, jnp.float32)
    if split:
        result = result * level_of(own_key, shape, split, -0.22, 0.18)
    return jnp.clip(result, -bound, bound).astype(kind)


def setup_inputs(seed: int = 0, part: int = 0) -> dict:
    seeds = jax.random.split(jax.random.key(seed), 9)
    part_splits = jax.random.split(jax.random.fold_in(seeds[8], part), 9)
    return {
        "ids": touch_ends(ranked(part_splits[0], (SEQ_LEN,), VOCAB, 2), jax.random.fold_in(part_splits[0], 3), 0, VOCAB - 1).astype(jnp.int32),
        "embed": bell_draw(seeds[1], (VOCAB, D), 1.0, 6.0),
        "norm_gain": jnp.clip(1.0 + 0.18 * jax.random.normal(seeds[2], (D,), jnp.float32), 0.1, 1.9),
        "w_in": bell_draw(seeds[3], (D, 3, D), D ** -0.5, 0.09375, ((0, 4), (2, 4))),
        "short_filter": bell_draw(seeds[4], (SHORT, 3, D), 0.6, 3.0, ((2, 4),), jnp.float32),
        "long_filter": bell_draw(seeds[5], (GROUPS, FL), 0.15, 1.0, ((0, 4),), jnp.float32),
        "skip_bias": bell_draw(seeds[6], (D,), 1.0, 4.0, ((0, 4),), jnp.float32),
        "w_out": bell_draw(seeds[7], (D, D), D ** -0.5, 0.09375, ((0, 4), (1, 4))),
    }


def reference(ids, embed, norm_gain, w_in, short_filter, long_filter, skip_bias, w_out):
    embedded = embed[ids]
    values = embedded.astype(jnp.float32)
    scaled = values * lax.rsqrt(lax.optimization_barrier(jnp.mean(values * values, axis=1, keepdims=True)) + 1e-06) * norm_gain
    normed = scaled.astype(jnp.bfloat16)
    projected = jnp.dot(normed, w_in.reshape(D, 3 * D), preferred_element_type=jnp.float32)
    projected = projected.astype(jnp.bfloat16).reshape(SEQ_LEN, 3, D)
    padded = jnp.concatenate([jnp.zeros((SHORT - 1, 3, D), jnp.float32), projected.astype(jnp.float32)], axis=0)
    mixed = jnp.zeros((SEQ_LEN, 3, D), jnp.float32)
    for offset in range(SHORT):
        mixed = mixed + short_filter[offset] * padded[SHORT - 1 - offset:SHORT - 1 - offset + SEQ_LEN]
    product = (mixed[:, 1, :] * mixed[:, 2, :]).astype(jnp.bfloat16)
    per_channel = jnp.repeat(long_filter, D // GROUPS, axis=0)
    upadded = jnp.concatenate([jnp.zeros((FL - 1, D), jnp.float32), product.astype(jnp.float32)], axis=0)

    def one_tap(offset, total):
        column = lax.dynamic_slice_in_dim(per_channel, offset, 1, 1)[:, 0]
        return total + column * lax.dynamic_slice_in_dim(upadded, FL - 1 - offset, SEQ_LEN, 0)
    conv = lax.fori_loop(0, FL, one_tap, jnp.zeros((SEQ_LEN, D), jnp.float32))
    gated = (mixed[:, 0, :] * (conv + skip_bias * product.astype(jnp.float32))).astype(jnp.bfloat16)
    update = jnp.dot(gated, w_out, preferred_element_type=jnp.float32)
    return (values + update).astype(jnp.bfloat16)
```

```python
import jax
import jax.numpy as jnp
from jax import lax
from jax.sharding import PartitionSpec as P

FL = 128
SHORT = 3


def rotate(value, axis, steps):
    count = lax.axis_size(axis)
    return lax.ppermute(value, axis, [(i, (i + steps) % count) for i in range(count)])


def in_order(blocks, index):
    count = len(blocks)
    if count == 1:
        return jnp.stack(blocks)
    line = blocks[::-1]
    twice = jnp.stack(line + line[:-1])
    return lax.dynamic_slice_in_dim(twice, count - 1 - index, count, 0)


def gather_rotating(value, axis):
    count = lax.axis_size(axis)
    blocks = [value] + [rotate(value, axis, r) for r in range(1, count)]
    return in_order(blocks, lax.axis_index(axis))


def onehot_rows(ids, vocab):
    index = lax.broadcasted_iota(jnp.int32, (1, vocab), 1)
    return (ids[:, None] == index).astype(jnp.bfloat16)


def on_device(ids, embed, norm_gain, w_in, short_filter, long_filter, skip_bias, w_out):
    tok = ids.shape[0]
    vocab, width = embed.shape
    depth, _, chans = w_in.shape
    sn = lax.axis_size("seq")
    s = lax.axis_index("seq")
    p = lax.axis_index("parts")
    pn = lax.axis_size("parts")
    fc = lax.axis_index(("fsdp", "chan"))
    sub = chans // sn
    total_tok = tok * sn

    rows = w_out.shape[0]
    share = rows // pn
    mine = lax.dynamic_slice_in_dim(w_out, p * share, share, 0)
    up_pairs = lambda j: [(i, i + 1) for i in range(j - 1, sn - 1)]
    down_pairs = lambda j: [(i, i - 1) for i in range(1, sn - j + 1)]
    up = [lax.ppermute(mine, "seq", up_pairs(1))]
    down = [lax.ppermute(mine, "seq", down_pairs(1))]

    all_ids = gather_rotating(ids, "seq").reshape(total_tok)

    vshare = vocab // pn
    table_rows = lax.dynamic_slice_in_dim(embed, p * vshare, vshare, 0)
    values = table_rows.astype(jnp.float32)
    inverse = lax.rsqrt(jnp.mean(values * values, axis=1, keepdims=True) + 1e-06)
    piece = lax.dynamic_slice_in_dim(table_rows, s * depth, depth, 1).astype(jnp.float32)
    gain = lax.dynamic_slice_in_dim(norm_gain, s * depth, depth, 0)
    normed = (piece * inverse * gain).astype(jnp.bfloat16)
    partial = jnp.einsum("vk,kic->ivc", normed, w_in, preferred_element_type=jnp.float32)
    summed = lax.dynamic_slice_in_dim(partial, s * sub, sub, 2)
    arrived = []
    for r in range(1, sn):
        out = lax.dynamic_slice_in_dim(partial, ((s + r) % sn) * sub, sub, 2)
        arrived.append(rotate(out.astype(jnp.bfloat16), "seq", r))
    for block in arrived:
        summed = summed + block.astype(jnp.float32)
    half = summed.astype(jnp.bfloat16)
    up[0], down[0], half = lax.optimization_barrier((up[0], down[0], half))

    for j in range(2, sn):
        up.append(lax.ppermute(up[-1], "seq", up_pairs(j)))
        down.append(lax.ppermute(down[-1], "seq", down_pairs(j)))

    table = gather_rotating(half, "parts")
    table = jnp.moveaxis(table, 0, 1).reshape(3, vocab, sub)

    hot = onehot_rows(all_ids, vocab)
    taps = lax.dynamic_slice_in_dim(short_filter, s * sub, sub, 2)
    mixed = []
    for i in range(3):
        projected = jnp.dot(hot, table[i], preferred_element_type=jnp.float32)
        padded = jnp.concatenate([jnp.zeros((SHORT - 1, sub), jnp.float32), projected], axis=0)
        total = jnp.zeros((total_tok, sub), jnp.float32)
        for offset in range(SHORT):
            begin = SHORT - 1 - offset
            total = total + taps[offset, i] * padded[begin : begin + total_tok]
        mixed.append(total)
    product = (mixed[1] * mixed[2]).astype(jnp.bfloat16)

    groups = long_filter.shape[0] // sn
    per_group = sub // groups
    filters = lax.dynamic_slice_in_dim(long_filter, s * groups, groups, 0)
    line = jnp.concatenate(
        [jnp.zeros((groups, 1), jnp.float32), filters[:, ::-1], jnp.zeros((groups, FL), jnp.float32)],
        axis=1,
    )
    band = jnp.tile(line, (1, FL))[:, : 2 * FL * FL].reshape(groups, FL, 2 * FL)
    blocks = total_tok // FL
    framed = jnp.concatenate([jnp.zeros((FL, sub), jnp.bfloat16), product], axis=0)
    tiles = framed.reshape(blocks + 1, FL, sub)
    window = jnp.concatenate([tiles[:-1], tiles[1:]], axis=1)
    window = window.astype(jnp.float32).reshape(blocks, 2 * FL, groups, per_group)
    conv = jnp.einsum("gts,bsgk->btgk", band, window, precision=lax.Precision.HIGHEST)
    conv = conv.reshape(total_tok, sub)
    bias = lax.dynamic_slice_in_dim(skip_bias, s * sub, sub, 0)
    gated = (mixed[0] * (conv + bias * product.astype(jnp.float32))).astype(jnp.bfloat16)

    parcels = [lax.dynamic_slice_in_dim(gated, s * tok, tok, 0)]
    for r in range(1, sn):
        parcel = lax.dynamic_slice_in_dim(gated, ((s + r) % sn) * tok, tok, 0)
        parcels.append(rotate(parcel, "seq", r))
    local = in_order(parcels, s)
    everyone = gather_rotating(gather_rotating(local, "fsdp"), "chan")
    columns = jnp.transpose(everyone, (3, 1, 0, 2, 4)).reshape(tok, width)

    hot_own = onehot_rows(ids, vocab)
    own_cols = lax.dynamic_slice_in_dim(embed, fc * chans, chans, 1)
    acc = jnp.dot(hot_own, own_cols, preferred_element_type=jnp.float32)

    acc = acc + jnp.dot(
        lax.dynamic_slice_in_dim(columns, s * rows, rows, 1), w_out,
        preferred_element_type=jnp.float32,
    )

    def across(value, valid):
        pairs = [
            (q * sn + i, ((q + 1) % pn) * sn + i) for q in range(pn) for i in range(sn) if valid(i)
        ]
        return lax.ppermute(value, ("parts", "seq"), pairs)

    other = (p + 1) % pn
    up_other = [across(v, lambda i, j=j: i >= j) for j, v in enumerate(up, 1)]
    down_other = [across(v, lambda i, j=j: i <= sn - 1 - j) for j, v in enumerate(down, 1)]
    for j in range(1, sn):
        source = (s - j) % sn
        for which, ups, downs in ((p, up, down), (other, up_other, down_other)):
            weights = jnp.where(s >= j, ups[j - 1], downs[sn - j - 1])
            start = source * rows + which * share
            acc = acc + jnp.dot(
                lax.dynamic_slice_in_dim(columns, start, share, 1), weights,
                preferred_element_type=jnp.float32,
            )
    return acc.astype(jnp.bfloat16)


def solution(mesh):
    assert mesh.shape["parts"] == 2
    in_specs = (
        P(("parts", "seq")),
        P(),
        P(),
        P("seq", None, ("fsdp", "chan")),
        P(None, None, ("fsdp", "chan")),
        P(("fsdp", "chan"), None),
        P(("fsdp", "chan")),
        P("seq", ("fsdp", "chan")),
    )
    out_specs = P(("parts", "seq"), ("fsdp", "chan"))
    return jax.shard_map(
        on_device, mesh=mesh, in_specs=in_specs, out_specs=out_specs, check_vma=False
    )
```

```python
import jax
import jax.numpy as jnp
from jax import lax
from jax.sharding import PartitionSpec as P

FL = 128
SHORT = 3


def rotate(value, axis, steps):
    count = lax.axis_size(axis)
    return lax.ppermute(value, axis, [(i, (i + steps) % count) for i in range(count)])


def in_order(blocks, index):
    count = len(blocks)
    if count == 1:
        return jnp.stack(blocks)
    line = blocks[::-1]
    twice = jnp.stack(line + line[:-1])
    return lax.dynamic_slice_in_dim(twice, count - 1 - index, count, 0)


def gather_rotating(value, axis):
    count = lax.axis_size(axis)
    blocks = [value] + [rotate(value, axis, r) for r in range(1, count)]
    return in_order(blocks, lax.axis_index(axis))


def onehot_rows(ids, vocab):
    index = lax.broadcasted_iota(jnp.int32, (1, vocab), 1)
    return (ids[:, None] == index).astype(jnp.bfloat16)


def on_device(ids, embed, norm_gain, w_in, short_filter, long_filter, skip_bias, w_out):
    tok = ids.shape[0]
    vocab, width = embed.shape
    depth, _, chans = w_in.shape
    sn = lax.axis_size("seq")
    s = lax.axis_index("seq")
    p = lax.axis_index("parts")
    pn = lax.axis_size("parts")
    fc = lax.axis_index(("fsdp", "chan"))
    sub = chans // sn
    total_tok = tok * sn

    rows = w_out.shape[0]
    share = rows // pn
    mine = lax.dynamic_slice_in_dim(w_out, p * share, share, 0)
    up_pairs = lambda j: [(i, i + 1) for i in range(j - 1, sn - 1)]
    down_pairs = lambda j: [(i, i - 1) for i in range(1, sn - j + 1)]
    up = [lax.ppermute(mine, "seq", up_pairs(1))]
    down = [lax.ppermute(mine, "seq", down_pairs(1))]

    all_ids = gather_rotating(ids, "seq").reshape(total_tok)

    vshare = vocab // pn
    table_rows = lax.dynamic_slice_in_dim(embed, p * vshare, vshare, 0)
    values = table_rows.astype(jnp.float32)
    inverse = lax.rsqrt(jnp.mean(values * values, axis=1, keepdims=True) + 1e-06)
    piece = lax.dynamic_slice_in_dim(table_rows, s * depth, depth, 1).astype(jnp.float32)
    gain = lax.dynamic_slice_in_dim(norm_gain, s * depth, depth, 0)
    normed = (piece * inverse * gain).astype(jnp.bfloat16)
    partial = jnp.einsum("vk,kic->ivc", normed, w_in, preferred_element_type=jnp.float32)
    summed = lax.dynamic_slice_in_dim(partial, s * sub, sub, 2)
    arrived = []
    for r in range(1, sn):
        out = lax.dynamic_slice_in_dim(partial, ((s + r) % sn) * sub, sub, 2)
        arrived.append(rotate(out.astype(jnp.bfloat16), "seq", r))
    for block in arrived:
        summed = summed + block.astype(jnp.float32)
    half = summed.astype(jnp.bfloat16)
    up[0], down[0], half = lax.optimization_barrier((up[0], down[0], half))

    for j in range(2, sn):
        up.append(lax.ppermute(up[-1], "seq", up_pairs(j)))
        down.append(lax.ppermute(down[-1], "seq", down_pairs(j)))

    table = gather_rotating(half, "parts")

    def across(value, valid):
        pairs = [
            (q * sn + i, ((q + 1) % pn) * sn + i) for q in range(pn) for i in range(sn) if valid(i)
        ]
        return lax.ppermute(value, ("parts", "seq"), pairs)

    other = (p + 1) % pn
    up_other = [across(v, lambda i, j=j: i >= j) for j, v in enumerate(up, 1)]
    down_other = [across(v, lambda i, j=j: i <= sn - 1 - j) for j, v in enumerate(down, 1)]
    tie = lax.optimization_barrier

    table = jnp.moveaxis(table, 0, 1).reshape(3, vocab, sub)

    hot = onehot_rows(all_ids, vocab)
    taps = lax.dynamic_slice_in_dim(short_filter, s * sub, sub, 2)
    mixed = []
    for i in range(3):
        projected = jnp.dot(hot, table[i], preferred_element_type=jnp.float32)
        padded = jnp.concatenate([jnp.zeros((SHORT - 1, sub), jnp.float32), projected], axis=0)
        total = jnp.zeros((total_tok, sub), jnp.float32)
        for offset in range(SHORT):
            begin = SHORT - 1 - offset
            total = total + taps[offset, i] * padded[begin : begin + total_tok]
        mixed.append(total)
    product = (mixed[1] * mixed[2]).astype(jnp.bfloat16)
    product, up[1:2], down[1:2] = tie((product, up[1:2], down[1:2]))

    groups = long_filter.shape[0] // sn
    per_group = sub // groups
    filters = lax.dynamic_slice_in_dim(long_filter, s * groups, groups, 0)
    line = jnp.concatenate(
        [jnp.zeros((groups, 1), jnp.float32), filters[:, ::-1], jnp.zeros((groups, FL), jnp.float32)],
        axis=1,
    )
    band = jnp.tile(line, (1, FL))[:, : 2 * FL * FL].reshape(groups, FL, 2 * FL)
    blocks = total_tok // FL
    framed = jnp.concatenate([jnp.zeros((FL, sub), jnp.bfloat16), product], axis=0)
    tiles = framed.reshape(blocks + 1, FL, sub)
    window = jnp.concatenate([tiles[:-1], tiles[1:]], axis=1)
    window = window.astype(jnp.float32).reshape(blocks, 2 * FL, groups, per_group)
    conv = jnp.einsum("gts,bsgk->btgk", band, window, precision=lax.Precision.HIGHEST)
    conv = conv.reshape(total_tok, sub)
    conv, up[2:], down[2:], up_other[:1], down_other[:1] = tie(
        (conv, up[2:], down[2:], up_other[:1], down_other[:1])
    )
    bias = lax.dynamic_slice_in_dim(skip_bias, s * sub, sub, 0)
    gated = (mixed[0] * (conv + bias * product.astype(jnp.float32))).astype(jnp.bfloat16)

    parcels = [lax.dynamic_slice_in_dim(gated, s * tok, tok, 0)]
    for r in range(1, sn):
        parcel = lax.dynamic_slice_in_dim(gated, ((s + r) % sn) * tok, tok, 0)
        parcels.append(rotate(parcel, "seq", r))
    local = in_order(parcels, s)
    local, up_other[1:2], down_other[1:2] = tie((local, up_other[1:2], down_other[1:2]))
    chip = gather_rotating(local, "fsdp")
    everyone = gather_rotating(chip, "chan")
    everyone, up_other[2:], down_other[2:] = tie((everyone, up_other[2:], down_other[2:]))
    columns = jnp.transpose(everyone, (3, 1, 0, 2, 4)).reshape(tok, width)

    hot_own = onehot_rows(ids, vocab)
    own_cols = lax.dynamic_slice_in_dim(embed, fc * chans, chans, 1)
    acc = jnp.dot(hot_own, own_cols, preferred_element_type=jnp.float32)

    acc = acc + jnp.dot(
        lax.dynamic_slice_in_dim(columns, s * rows, rows, 1), w_out,
        preferred_element_type=jnp.float32,
    )

    for j in range(1, sn):
        source = (s - j) % sn
        for which, ups, downs in ((p, up, down), (other, up_other, down_other)):
            weights = jnp.where(s >= j, ups[j - 1], downs[sn - j - 1])
            start = source * rows + which * share
            acc = acc + jnp.dot(
                lax.dynamic_slice_in_dim(columns, start, share, 1), weights,
                preferred_element_type=jnp.float32,
            )
    return acc.astype(jnp.bfloat16)


def solution(mesh):
    assert mesh.shape["parts"] == 2
    in_specs = (
        P(("parts", "seq")),
        P(),
        P(),
        P("seq", None, ("fsdp", "chan")),
        P(None, None, ("fsdp", "chan")),
        P(("fsdp", "chan"), None),
        P(("fsdp", "chan")),
        P("seq", ("fsdp", "chan")),
    )
    out_specs = P(("parts", "seq"), ("fsdp", "chan"))
    return jax.shard_map(
        on_device, mesh=mesh, in_specs=in_specs, out_specs=out_specs, check_vma=False
    )
```
